512 devices in a mesh: dp: 64 (over y, z), mix: 8 (over x, core).
Axes of the slice: x: 4, y: 8, z: 8, core: 2. Of those that a mesh axis runs over, the one named last changes fastest.
Arguments:
- matrix: float32 [131072, 1024], P(('dp', 'mix'))
- counts: int32 [64, 8], P('dp'), may hold values from 0 to 256, as said below
- sign_bits: int32 [131072], P(('dp', 'mix')), may hold values from 0 to 1
- samples: int32 [64, 32], P('dp'), may hold values from 0 to 1023
- gaussian: float32 [1024, 64], replicated, may hold values from -6 to 6
Outputs:
- leverage: float32 [131072], P(('dp', 'mix'))
The draws below stay inside these ranges and needn't reach their ends.
Inputs may be any that keep to these rules, and one draw needn't show every extreme that they name: In each dp index g, the counts of mix indices 0 to m - 1 sum to m * 128 plus a number of magnitude at most 64, which reaches that magnitude for some m in every g; all 8 counts sum to 1024.
All inputs are finite; a program needn't handle non-finite values.
Results may differ from the reference program's by a relative error of at most 0.0003.
Values sent between devices are 32-bit elements; how exact they have to be, the bound alone decides.
A program may use at most 64 MiB of HBM per device.

```python
import math
import jax
import jax.numpy as jnp
from jax import lax

NC = 1024
NG = 64
SLOTS = 128
CAPACITY = 256
GROUP = 1024
ROWS = 131072
TOTAL = 65536
SAMPLES = 2048
PICKS = 32
N_DP = 64
N_MIX = 8


def draw_matrix(key, part):
    subkeys = jax.random.split(key, 3)
    row_scale = jnp.exp(jax.random.uniform(subkeys[1], (ROWS, 1), jnp.float32) * math.log(10.0))
    col_scale = jnp.exp(jax.random.uniform(subkeys[2], (1, NC), jnp.float32) * math.log(10.0))
    entries = jax.random.normal(subkeys[0], (ROWS, NC), jnp.float32)
    scaled = entries * row_scale * col_scale
    return scaled.astype(jnp.float32)


def draw_counts(key, part):
    subkeys = jax.random.split(jax.random.fold_in(key, 17), 3)
    half_slots = SLOTS // 2
    inner = N_MIX - 1
    drift = jax.random.randint(subkeys[0], (N_DP, inner), -half_slots, half_slots + 1).astype(jnp.int32)
    position = jnp.arange(inner, dtype=jnp.int32)[None, :]
    if N_MIX >= 3:
        lowest = jax.random.randint(subkeys[1], (N_DP, 1), 0, inner - 1).astype(jnp.int32)
        drift = jnp.where(position == lowest, -half_slots, drift)
        drift = jnp.where(position == lowest + 1, half_slots, drift)
    else:
        sign_pick = 2 * jax.random.randint(subkeys[2], (N_DP, 1), 0, 2).astype(jnp.int32) - 1
        drift = jnp.where(position == 0, sign_pick * half_slots, drift)
    zeros = jnp.zeros((N_DP, 1), jnp.int32)
    full = jnp.concatenate([zeros, drift.astype(jnp.int32), zeros], axis=1)
    result = SLOTS + full[:, 1:] - full[:, :-1]
    return result.astype(jnp.int32)


def set_ends(values, rng, smallest, top_value):
    index_at = [jax.random.randint(jax.random.fold_in(rng, axis), (), 0, length) for axis, length in enumerate(values.shape)]
    main_axis = values.shape.index(max(values.shape))
    neighbour = index_at[:main_axis] + [(index_at[main_axis] + 1) % values.shape[main_axis]] + index_at[main_axis + 1:]
    return values.at[tuple(index_at)].set(smallest).at[tuple(neighbour)].set(top_value)


def bell_draw(rng, extent, spread, bound, kind=jnp.bfloat16):
    return jnp.clip(spread * jax.random.normal(rng, extent, jnp.float32), -bound, bound).astype(kind)


def setup_inputs(seed: int = 0) -> dict:
    seeds = jax.random.split(jax.random.key(seed), 6)
    return {
        "matrix": draw_matrix(jax.random.fold_in(seeds[5], 71), 0),
        "counts": draw_counts(jax.random.fold_in(seeds[5], 71), 0),
        "sign_bits": set_ends(jax.random.randint(seeds[2], (ROWS,), 0, 2), jax.random.fold_in(seeds[2], 1), 0, 1).astype(jnp.int32),
        "samples": set_ends(jax.random.randint(seeds[3], (N_DP, PICKS), 0, GROUP), jax.random.fold_in(seeds[3], 1), 0, GROUP - 1).astype(jnp.int32),
        "gaussian": bell_draw(seeds[4], (NC, NG), 1.0, 6.0, jnp.float32),
    }


def hadamard(row_ids, col_ids):
    correlation = jnp.bitwise_and(row_ids[:, None], col_ids[None, :])
    parity = jnp.zeros(correlation.shape, jnp.int32)
    for bit_number in range(16):
        parity = jnp.bitwise_xor(parity, jnp.bitwise_and(jnp.right_shift(correlation, bit_number), 1))
    return (1 - 2 * parity).astype(jnp.float32)

def reference(matrix, counts, sign_bits, samples, gaussian):
    slot_ids = jnp.arange(CAPACITY, dtype=jnp.int32)
    valid_rows = slot_ids[None, None, :] < counts[:, :, None]
    blocks = matrix.reshape(N_DP, N_MIX, CAPACITY, NC)
    sign_values = (2 * sign_bits - 1).astype(jnp.float32).reshape(N_DP, N_MIX, CAPACITY)
    sketch_scale = 1.0 / math.sqrt(GROUP * PICKS)

    def group_sketch(pieces):
        device_block, sign_block, valid_block, count_row, picked = pieces
        signed = jnp.where(valid_block[:, :, None], device_block * sign_block[:, :, None], 0.0)
        row_ends = jnp.cumsum(count_row).astype(jnp.int32)
        starts = (row_ends - count_row).astype(jnp.int32)
        logical = jnp.arange(GROUP, dtype=jnp.int32)
        owner_dev = lax.optimization_barrier(jnp.sum((logical[:, None] >= row_ends[None, :]).astype(jnp.int32), axis=1)).astype(jnp.int32)
        local_row = (logical - starts[owner_dev]).astype(jnp.int32)
        gathered = signed.reshape(N_MIX * CAPACITY, NC)[owner_dev * CAPACITY + local_row]
        hadamard_rows = hadamard(picked, logical)
        return jnp.dot(hadamard_rows, gathered, precision=lax.Precision.HIGHEST) * sketch_scale
    sketch = lax.map(group_sketch, (blocks, sign_values, valid_rows, counts, samples))
    all_sketch = sketch.reshape(SAMPLES, NC)
    gram_matrix = jnp.dot(all_sketch.T, all_sketch, precision=lax.Precision.HIGHEST)
    factor_lower = jnp.linalg.cholesky(gram_matrix)
    solved = jax.scipy.linalg.solve_triangular(factor_lower, gaussian, trans=1, lower=True)
    norm_factor = TOTAL / (NC * NG)

    def device_leverage(pieces):
        device_block, valid_block = pieces
        masked = jnp.where(valid_block[:, None], device_block, 0.0)
        projected = jnp.dot(masked, solved, precision=lax.Precision.HIGHEST)
        return lax.optimization_barrier(jnp.sum(projected * projected, axis=1)) * norm_factor
    leverage = lax.map(device_leverage, (matrix.reshape(N_DP * N_MIX, CAPACITY, NC), valid_rows.reshape(N_DP * N_MIX, CAPACITY)))
    return leverage.reshape(ROWS)
```

```python
import functools
import math

import jax
import jax.numpy as jnp
from jax import lax
from jax.experimental import pallas as pl
from jax.experimental.pallas import tpu as pltpu
from jax.sharding import PartitionSpec as P

HI = lax.Precision.HIGHEST
NN = (((1,), (0,)), ((), ()))
NT = (((1,), (1,)), ((), ()))
TN = (((0,), (0,)), ((), ()))
MESH = pl.DeviceIdType.MESH


def gram_kernel(n_mix, n, hs_ref, x_ref, g_ref, part, r1, s_all, w, r3, q, r4, f, *sems):
    (s1, v1, s2, v2, s3, v3, s4, v4, s5, v5, s6, v6, s7, v7, local) = sems
    dp, m = lax.axis_index("dp"), lax.axis_index("mix")
    y, z = dp // n, dp % n
    core = m % 2
    n_off = n_mix // 2 + 1
    piece = 128 // (2 * n)

    def mix_peer(d):
        return (dp, (m + d) % n_mix)

    def y_peer(d):
        return (((y + d) % n) * n + z, m)

    def z_peer(d):
        return (y * n + (z + d) % n, m)

    barrier = pltpu.get_barrier_semaphore()
    for d in range(1, n_mix):
        pl.semaphore_signal(barrier, inc=1, device_id=mix_peer(d), device_id_type=MESH)
    for d in range(1, n):
        pl.semaphore_signal(barrier, inc=1, device_id=y_peer(d), device_id_type=MESH)
        pl.semaphore_signal(barrier, inc=1, device_id=z_peer(d), device_id_type=MESH)

    def send(src, dst, ssem, rsem, peer):
        copy = pltpu.make_async_remote_copy(src_ref=src, dst_ref=dst, send_sem=ssem, recv_sem=rsem,
                                            device_id=peer, device_id_type=MESH)
        copy.start()
        return copy

    product = lax.dot_general(hs_ref[...], x_ref[...], NN, precision=HI, preferred_element_type=jnp.float32)
    product = product * (1.0 / math.sqrt(n_mix * 128 * hs_ref.shape[0]))
    for b in range(n_mix):
        part[b] = product[:, 128 * b:128 * b + 128]
    pl.semaphore_wait(barrier, n_mix - 1 + 2 * (n - 1))
    sent = []

    got = []
    for d in range(1, n_mix):
        p = (m + d) % n_mix
        got.append(send(part.at[p], r1.at[m], s1.at[d], v1.at[d], mix_peer(d)))
    r1[m] = part[m]
    for copy in got:
        copy.wait_recv()
    sent += got
    s_all[m] = functools.reduce(jnp.add, [r1[b] for b in range(n_mix)])
    got = []
    for d in range(1, n_mix):
        got.append(send(s_all.at[m], s_all.at[m], s2.at[d], v2.at[d], mix_peer(d)))
    for copy in got:
        copy.wait_recv()
    sent += got

    for o in range(n_off):
        b = (m + o) % n_mix
        low, high = jnp.minimum(m, b), jnp.maximum(m, b)
        tile = lax.dot_general(s_all[high], s_all[low], TN, precision=HI, preferred_element_type=jnp.float32)
        for h in range(2):
            for p in range(n):
                r = (h * n + p) * piece
                w[h, p, o] = tile[r:r + piece]

    got = []
    for d in range(1, n):
        got.append(send(w.at[0, (y + d) % n], r3.at[0, y], s3.at[0, d], v3.at[0, d], y_peer(d)))
        got.append(send(w.at[1, (z + d) % n], r3.at[1, z], s3.at[1, d], v3.at[1, d], z_peer(d)))
    r3[0, y] = w[0, y]
    r3[1, z] = w[1, z]
    for copy in got:
        copy.wait_recv()
    sent += got
    for h in range(2):
        q[h] = functools.reduce(jnp.add, [r3[h, p] for p in range(n)])
    got = []
    for d in range(1, n):
        got.append(send(q.at[0], r4.at[0, z], s4.at[0, d], v4.at[0, d], z_peer(d)))
        got.append(send(q.at[1], r4.at[1, y], s4.at[1, d], v4.at[1, d], y_peer(d)))
    r4[0, z] = q[0]
    r4[1, y] = q[1]
    for copy in got:
        copy.wait_recv()
    sent += got
    for h in range(2):
        f[h, m] = functools.reduce(jnp.add, [r4[h, p] for p in range(n)])

    got = []
    for d in range(1, n_mix):
        for h in range(2):
            got.append(send(f.at[h, m], f.at[h, m], s5.at[h, d], v5.at[h, d], mix_peer(d)))
    for copy in got:
        copy.wait_recv()
    sent += got
    place = y + core * (z - y)
    sibling = (dp, m + 1 - 2 * core)
    got = []
    for d in range(1, n):
        peer = (((y + d * (1 - core)) % n) * n + (z + d * core) % n, m)
        got.append(send(f.at[core], g_ref.at[core, place], s6.at[d], v6.at[d], peer))
    own = pltpu.make_async_copy(f.at[core], g_ref.at[core, place], local)
    own.start()
    across = [send(f.at[core], g_ref.at[core, place], s7.at[0], v7.at[0], sibling)]
    for d in range(1, n):
        got[d - 1].wait_recv()
        slot = (place + n - d) % n
        across.append(send(g_ref.at[core, slot], g_ref.at[core, slot], s7.at[d], v7.at[d], sibling))
    sent += got + across
    own.wait()
    for copy in across:
        copy.wait_recv()
    for copy in sent:
        copy.wait_send()


def gram_call(n_mix, n, hs, x):
    vm = pl.BlockSpec(memory_space=pltpu.VMEM)
    n_off, piece, k = n_mix // 2 + 1, 128 // (2 * n), hs.shape[0]
    f32 = jnp.float32
    dma = pltpu.SemaphoreType.DMA
    pair = lambda *s: [dma(s), dma(s)]
    return pl.pallas_call(
        functools.partial(gram_kernel, n_mix, n),
        out_shape=jax.ShapeDtypeStruct((2, n, n_mix, n_off, piece, 128), f32),
        in_specs=[vm] * 2, out_specs=vm,
        scratch_shapes=[
            pltpu.VMEM((n_mix, k, 128), f32), pltpu.VMEM((n_mix, k, 128), f32), pltpu.VMEM((n_mix, k, 128), f32),
            pltpu.VMEM((2, n, n_off, piece, 128), f32), pltpu.VMEM((2, n, n_off, piece, 128), f32),
            pltpu.VMEM((2, n_off, piece, 128), f32), pltpu.VMEM((2, n, n_off, piece, 128), f32),
            pltpu.VMEM((2, n_mix, n_off, piece, 128), f32),
            *pair(n_mix), *pair(n_mix), *pair(2, n), *pair(2, n), *pair(2, n_mix), *pair(n), *pair(n), dma(())],
        compiler_params=pltpu.CompilerParams(collective_id=0, has_side_effects=True, vmem_limit_bytes=32 * 1024 * 1024),
    )(hs, x)


def mm(a, b, dims):
    return lax.dot_general(a, b, dims, precision=HI, preferred_element_type=jnp.float32)


def factor_inverse(d_ref, t_ref):
    shape = (8, 128)
    lane = lax.broadcasted_iota(jnp.int32, shape, 1)
    sub = lax.broadcasted_iota(jnp.int32, shape, 0)
    tiles = [d_ref[8 * t:8 * t + 8, :] for t in range(16)]
    lanes_of = lambda x, c: jnp.broadcast_to(x[:, c:c + 1], shape)
    rows_of = lambda x, r: jnp.broadcast_to(x[r:r + 1, :], shape)
    for t in range(16):
        base = 8 * t
        own = tiles[t]
        cols = [lanes_of(own, base + j) for j in range(8)]
        e = [[rows_of(cols[j], i) for j in range(i + 1)] for i in range(8)]
        row = [rows_of(own, i) for i in range(8)]
        piv, inv, low = [], [], {}
        for k in range(8):
            piv.append(e[k][k])
            inv.append(1.0 / e[k][k])
            for i in range(k + 1, 8):
                low[i, k] = e[i][k] * inv[k]
            for i in range(k + 1, 8):
                for j in range(k + 1, i + 1):
                    e[i][j] = e[i][j] - low[i, k] * e[j][k]
        tri = {}
        for i in range(8):
            for j in range(i):
                acc = low[i, j]
                for k in range(j + 1, i):
                    acc = acc + low[i, k] * tri[k, j]
                tri[i, j] = -acc
        inside = (lane >= base) & (lane < base + 8)
        rows = []
        for i in range(8):
            acc = row[i]
            patt = jnp.where(lane == base + i, 1.0, 0.0)
            for k in range(i):
                acc = acc + tri[i, k] * row[k]
                patt = jnp.where(lane == base + k, tri[i, k], patt)
            rows.append(jnp.where(inside, patt, acc))
        out = jnp.zeros(shape, jnp.float32)
        for i in range(8):
            out = jnp.where(sub == i, rows[i] * lax.rsqrt(piv[i]), out)
        t_ref[base:base + 8, :] = jnp.where(lane <= base + sub, out, 0.0)
        scaled = [rows[k] * inv[k] for k in range(8)]
        for u in range(t + 1, 16):
            c0 = [lanes_of(tiles[u], base + j) for j in range(8)]
            acc = jnp.where(inside, 0.0, tiles[u])
            for k in range(8):
                c = c0[k]
                for j in range(k):
                    c = c + tri[k, j] * c0[j]
                acc = acc - c * scaled[k]
            tiles[u] = acc


def chol_kernel(g_ref, gt_ref, x_ref, keep_ref, o_ref, a_ref, t_ref, y_ref, d_ref, acc_ref, xt_ref):
    nb = 8
    for i in range(nb):
        for j in range(i + 1):
            m, o = (j, i - j) if i - j <= 4 else (i, 8 - i + j)
            for h in range(2):
                for p in range(8):
                    r = i * 128 + h * 64 + p * 8
                    a_ref[r:r + 8, j * 128:j * 128 + 128] = g_ref[h, p, m, o]
    y_ref[...] = jnp.zeros_like(y_ref)

    def step(kb, carry):
        at = pl.multiple_of(kb * 128, 128)
        d_ref[...] = a_ref[pl.ds(at, 128), pl.ds(at, 128)]
        factor_inverse(d_ref, t_ref.at[kb])
        tri = t_ref[kb]
        for c in range(nb):
            @pl.when(kb == c)
            def _():
                if c:
                    y_ref[128 * c:128 * c + 128, :128 * c] = mm(tri, a_ref[128 * c:128 * c + 128, :128 * c], NN)
                if c < nb - 1:
                    lo = 128 * (c + 1)
                    for i in range(c + 1, nb):
                        a_ref[128 * i:128 * i + 128, 128 * c:lo] = mm(a_ref[128 * i:128 * i + 128, 128 * c:lo], tri, NT)
                    for i in range(c + 1, nb):
                        hi = 128 * (i + 1)
                        v = a_ref[128 * i:hi, 128 * c:lo]
                        a_ref[128 * i:hi, lo:hi] = a_ref[128 * i:hi, lo:hi] - mm(v, a_ref[lo:hi, 128 * c:lo], NT)
        return carry

    lax.fori_loop(0, nb, step, 0)
    acc_ref[...] = gt_ref[...]
    for i in range(nb - 1, -1, -1):
        s = slice(128 * i, 128 * i + 128)
        head = acc_ref[:, s]
        xt_ref[:, s] = mm(head, t_ref[i], NN)
        if i:
            acc_ref[:, :128 * i] = acc_ref[:, :128 * i] - mm(head, y_ref[s, :128 * i], NN)
    proj = mm(xt_ref[...], x_ref[...], NT)
    o_ref[...] = jnp.where(keep_ref[...] > 0, jnp.sum(proj * proj, axis=0, keepdims=True), 0.0)


def chol_call(g, gt, x, keep):
    vm = pl.BlockSpec(memory_space=pltpu.VMEM)
    return pl.pallas_call(
        chol_kernel,
        out_shape=jax.ShapeDtypeStruct((1, 256), jnp.float32),
        in_specs=[vm] * 4, out_specs=vm,
        scratch_shapes=[pltpu.VMEM((1024, 1024), jnp.float32), pltpu.VMEM((8, 128, 128), jnp.float32),
                        pltpu.VMEM((1024, 1024), jnp.float32), pltpu.VMEM((128, 128), jnp.float32),
                        pltpu.VMEM((64, 1024), jnp.float32), pltpu.VMEM((64, 1024), jnp.float32)],
        compiler_params=pltpu.CompilerParams(vmem_limit_bytes=48 * 1024 * 1024),
    )(g, gt, x, keep)


def shards(matrix, counts, sign_bits, samples, gaussian):
    capacity = matrix.shape[0]
    n_mix, n_dp = lax.axis_size("mix"), lax.axis_size("dp")
    mix_index = lax.axis_index("mix")
    member = jnp.arange(n_mix, dtype=jnp.int32)
    first_row = jnp.sum(jnp.where(member < mix_index, counts[0], 0))
    own_count = jnp.sum(jnp.where(member == mix_index, counts[0], 0))
    slots = jnp.arange(capacity, dtype=jnp.int32)
    kept = slots < own_count
    common = jnp.bitwise_and(samples[0][:, None], (first_row + slots)[None, :])
    odd = jnp.bitwise_and(lax.population_count(common), 1)
    signs = (1 - 2 * odd) * (2 * sign_bits - 1)[None, :]
    table = jnp.where(kept[None, :], signs, 0).astype(jnp.float32)
    grams = gram_call(n_mix, math.isqrt(n_dp), table, matrix)
    keep = kept.astype(jnp.int32)[None, :]
    return chol_call(grams, gaussian.T, matrix, keep)[0]


def solution(mesh):
    in_specs = (P(("dp", "mix"), None), P("dp", None), P(("dp", "mix")), P("dp", None), P())
    out_specs = P(("dp", "mix"))
    return jax.shard_map(shards, mesh=mesh, in_specs=in_specs, out_specs=out_specs, check_vma=False)
```

```python
import functools
import math

import jax
import jax.numpy as jnp
from jax import lax
from jax.experimental import pallas as pl
from jax.experimental.pallas import tpu as pltpu
from jax.sharding import PartitionSpec as P

HI = lax.Precision.HIGHEST
NN = (((1,), (0,)), ((), ()))
NT = (((1,), (1,)), ((), ()))
TN = (((0,), (0,)), ((), ()))
MESH = pl.DeviceIdType.MESH
CHUNKS = 4


def own_rows(counts_ref, n_mix):
    m = lax.axis_index("mix")
    first, count = jnp.int32(0), jnp.int32(0)
    for i in range(n_mix):
        first = first + jnp.where(i < m, counts_ref[0, i], 0)
        count = count + jnp.where(i == m, counts_ref[0, i], 0)
    return first, count


def gram_kernel(n_mix, n, counts_ref, samples_ref, bits_ref, x_ref, g_ref,
                part, r1, s_all, w, r3, q, r4, f, *sems):
    (s1, v1, s2, v2, s3, v3, s4, v4, s5, v5, s6, v6, s7, v7, local) = sems
    dp, m = lax.axis_index("dp"), lax.axis_index("mix")
    y, z = dp // n, dp % n
    x, core = m // 2, m % 2
    nx = n_mix // 2
    n_off = n_mix // 2 + 1
    piece = 128 // (2 * n)
    capacity, picks = x_ref.shape[0], samples_ref.shape[1]

    def mix_peer(d):
        return (dp, (m + d) % n_mix)

    def y_peer(d):
        return (((y + d) % n) * n + z, m)

    def z_peer(d):
        return (y * n + (z + d) % n, m)

    barrier = pltpu.get_barrier_semaphore()
    for d in range(1, n_mix):
        pl.semaphore_signal(barrier, inc=1, device_id=mix_peer(d), device_id_type=MESH)
    for d in range(1, n):
        pl.semaphore_signal(barrier, inc=1, device_id=y_peer(d), device_id_type=MESH)
        pl.semaphore_signal(barrier, inc=1, device_id=z_peer(d), device_id_type=MESH)

    def send(src, dst, ssem, rsem, peer):
        copy = pltpu.make_async_remote_copy(src_ref=src, dst_ref=dst, send_sem=ssem, recv_sem=rsem,
                                            device_id=peer, device_id_type=MESH)
        copy.start()
        return copy

    first, count = own_rows(counts_ref, n_mix)
    slot = lax.broadcasted_iota(jnp.int32, (8, capacity), 1)
    row = lax.broadcasted_iota(jnp.int32, (8, capacity), 0)
    sign = jnp.where(slot < count, 2 * bits_ref[...] - 1, 0)
    table = []
    for base in range(0, picks, 8):
        sample = jnp.zeros((8, capacity), jnp.int32)
        for i in range(8):
            sample = jnp.where(row == i, samples_ref[0, base + i], sample)
        odd = jnp.bitwise_and(sample, first + slot)
        for shift in (8, 4, 2, 1):
            odd = jnp.bitwise_xor(odd, jnp.right_shift(odd, shift))
        table.append(jnp.where(jnp.bitwise_and(odd, 1) == 1, -sign, sign))
    table = jnp.concatenate(table, axis=0).astype(jnp.float32).astype(jnp.bfloat16)
    scale = 1.0 / math.sqrt(n_mix * 128 * picks)
    for b in range(n_mix):
        rest = x_ref[:, 128 * b:128 * b + 128]
        total = None
        for _ in range(3):
            term = rest.astype(jnp.bfloat16)
            rest = rest - term.astype(jnp.float32)
            product = lax.dot_general(table, term, NN, preferred_element_type=jnp.float32)
            total = product if total is None else total + product
        part[b] = total * scale
    pl.semaphore_wait(barrier, n_mix - 1 + 2 * (n - 1))
    sent = []

    got = []
    for d in range(1, n_mix):
        p = (m + d) % n_mix
        got.append(send(part.at[p], r1.at[m], s1.at[d], v1.at[d], mix_peer(d)))
    r1[m] = part[m]
    for copy in got:
        copy.wait_recv()
    sent += got
    s_all[m] = functools.reduce(jnp.add, [r1[b] for b in range(n_mix)])
    got = []
    for d in range(1, n_mix):
        got.append(send(s_all.at[m], s_all.at[m], s2.at[d], v2.at[d], mix_peer(d)))
    for copy in got:
        copy.wait_recv()
    sent += got

    for o in range(n_off):
        b = (m + o) % n_mix
        low, high = jnp.minimum(m, b), jnp.maximum(m, b)
        tile = lax.dot_general(s_all[high], s_all[low], TN, precision=HI, preferred_element_type=jnp.float32)
        for h in range(2):
            for p in range(n):
                r = (h * n + p) * piece
                w[h, p, o] = tile[r:r + piece]

    got = []
    for d in range(1, n):
        got.append(send(w.at[0, (y + d) % n], r3.at[0, y], s3.at[0, d], v3.at[0, d], y_peer(d)))
        got.append(send(w.at[1, (z + d) % n], r3.at[1, z], s3.at[1, d], v3.at[1, d], z_peer(d)))
    r3[0, y] = w[0, y]
    r3[1, z] = w[1, z]
    for copy in got:
        copy.wait_recv()
    sent += got
    for h in range(2):
        q[h] = functools.reduce(jnp.add, [r3[h, p] for p in range(n)])
    got = []
    for d in range(1, n):
        got.append(send(q.at[0], r4.at[0, z], s4.at[0, d], v4.at[0, d], z_peer(d)))
        got.append(send(q.at[1], r4.at[1, y], s4.at[1, d], v4.at[1, d], y_peer(d)))
    r4[0, z] = q[0]
    r4[1, y] = q[1]
    for copy in got:
        copy.wait_recv()
    sent += got
    for h in range(2):
        f[h, m] = functools.reduce(jnp.add, [r4[h, p] for p in range(n)])

    got = []
    for d in range(nx):
        column = ((x + d) % nx) * 2
        if d:
            got.append(send(f.at[core, m], f.at[core, m], s5.at[0, d], v5.at[0, d], (dp, column + core)))
        got.append(send(f.at[1 - core, m], f.at[1 - core, m], s5.at[1, d], v5.at[1, d], (dp, column + 1 - core)))
    for copy in got:
        copy.wait_recv()
    sent += got

    place = y + core * (z - y)
    sibling = (dp, m + 1 - 2 * core)
    up = (((y + 1 - core) % n) * n + (z + core) % n, m)
    down = (((y + n - 1 + core) % n) * n + (z + n - core) % n, m)
    width = n_mix // CHUNKS
    far = n // 2
    own = pltpu.make_async_copy(f.at[core], g_ref.at[core, place], local)
    own.start()

    def relay(way, d, c, source):
        at = (place + (n - d if way == 0 else d)) % n
        rows = pl.ds(c * width, width)
        dst = g_ref.at[core, at, rows]
        return send(source if d == 0 else dst, dst, s6.at[way, d, c], v6.at[way, d, c], (up, down)[way])

    def goes(way, d, c):
        return d < far - 1 or (d == far - 1 and (c < CHUNKS // 2) == (way == 0))

    moves = {}
    across = []
    for c in range(CHUNKS):
        for way in range(2):
            if goes(way, 0, c):
                moves[way, 0, c] = relay(way, 0, c, f.at[core, pl.ds(c * width, width)])
    across.append(send(f.at[core], g_ref.at[core, place], s7.at[0, 0, 0], v7.at[0, 0, 0], sibling))
    for d in range(1, far + 1):
        for c in range(CHUNKS):
            for way in range(2):
                if goes(way, d - 1, c):
                    moves[way, d - 1, c].wait_recv()
                    if goes(way, d, c):
                        moves[way, d, c] = relay(way, d, c, None)
                    at = (place + (n - d if way == 0 else d)) % n
                    block = g_ref.at[core, at, pl.ds(c * width, width)]
                    across.append(send(block, block, s7.at[way, d, c], v7.at[way, d, c], sibling))
    own.wait()
    for copy in across:
        copy.wait_recv()
    for copy in sent + across + list(moves.values()):
        copy.wait_send()


def gram_call(n_mix, n, counts, samples, bits, x):
    vm = pl.BlockSpec(memory_space=pltpu.VMEM)
    sm = pl.BlockSpec(memory_space=pltpu.SMEM)
    n_off, piece, k = n_mix // 2 + 1, 128 // (2 * n), samples.shape[1]
    f32 = jnp.float32
    dma = pltpu.SemaphoreType.DMA
    pair = lambda *s: [dma(s), dma(s)]
    return pl.pallas_call(
        functools.partial(gram_kernel, n_mix, n),
        out_shape=jax.ShapeDtypeStruct((2, n, n_mix, n_off, piece, 128), f32),
        in_specs=[sm, sm, vm, vm], out_specs=vm,
        scratch_shapes=[
            pltpu.VMEM((n_mix, k, 128), f32), pltpu.VMEM((n_mix, k, 128), f32), pltpu.VMEM((n_mix, k, 128), f32),
            pltpu.VMEM((2, n, n_off, piece, 128), f32), pltpu.VMEM((2, n, n_off, piece, 128), f32),
            pltpu.VMEM((2, n_off, piece, 128), f32), pltpu.VMEM((2, n, n_off, piece, 128), f32),
            pltpu.VMEM((2, n_mix, n_off, piece, 128), f32),
            *pair(n_mix), *pair(n_mix), *pair(2, n), *pair(2, n), *pair(2, n_mix // 2),
            *pair(2, n // 2 + 1, CHUNKS), *pair(2, n // 2 + 1, CHUNKS), dma(())],
        compiler_params=pltpu.CompilerParams(collective_id=0, has_side_effects=True, vmem_limit_bytes=32 * 1024 * 1024),
    )(counts, samples, bits, x)


def mm(a, b, dims):
    return lax.dot_general(a, b, dims, precision=HI, preferred_element_type=jnp.float32)


def split(x):
    high = x.astype(jnp.bfloat16)
    rest = x - high.astype(jnp.float32)
    mid = rest.astype(jnp.bfloat16)
    return high, mid, (rest - mid.astype(jnp.float32)).astype(jnp.bfloat16)


def left_terms(x):
    high, mid, low = split(x)
    return jnp.concatenate([high, high, mid, high, low, mid], axis=1)


def right_terms(x):
    high, mid, low = split(x)
    return jnp.concatenate([high, mid, high, low, high, mid], axis=1)


def wide(a, b):
    return lax.dot_general(a, b, NT, preferred_element_type=jnp.float32)


def mm3(a, b, dims):
    ah, bh = a.astype(jnp.bfloat16), b.astype(jnp.bfloat16)
    al = (a - ah.astype(jnp.float32)).astype(jnp.bfloat16)
    bl = (b - bh.astype(jnp.float32)).astype(jnp.bfloat16)
    dot = functools.partial(lax.dot_general, dimension_numbers=dims, preferred_element_type=jnp.float32)
    return dot(ah, bh) + (dot(ah, bl) + dot(al, bh))


def factor_inverse(d_ref, t_ref, zero):
    shape = (8, 128)
    lane = lax.broadcasted_iota(jnp.int32, shape, 1)
    sub = lax.broadcasted_iota(jnp.int32, shape, 0)
    tiles = [d_ref[8 * t:8 * t + 8, :] for t in range(16)]
    lanes_of = lambda x, c: jnp.broadcast_to(x[:, c:c + 1], shape)
    rows_of = lambda x, r: jnp.broadcast_to(x[r:r + 1, :], shape)
    cols = [lanes_of(tiles[0], j) + zero for j in range(8)]
    for t in range(16):
        base = 8 * t
        inside = (lane >= base) & (lane < base + 8)
        below = [[lanes_of(tiles[u], base + j) for j in range(8)] for u in range(t + 1, 16)]
        if t < 15:
            x = [b + zero for b in below[0]]
            ahead = [lanes_of(tiles[t + 1], base + 8 + j) + zero for j in range(8)]
        row = jnp.where(inside, jnp.where(lane == base + sub, 1.0, 0.0), tiles[t])
        low, inv_col, piv_col = {}, zero, zero + 1.0
        for k in range(8):
            pivot = rows_of(cols[k], k)
            inv = 1.0 / pivot
            factor = cols[k] * inv
            for j in range(k + 1, 8):
                cols[j] = cols[j] - factor * rows_of(cols[k], j)
                low[j, k] = rows_of(factor, j)
            inv_col = jnp.where(sub == k, inv, inv_col)
            piv_col = jnp.where(sub == k, pivot, piv_col)
            if k < 7:
                row = row - jnp.where(sub > k, factor, 0.0) * rows_of(row, k)
            if t < 15:
                y = x[k] * inv
                ahead = [ahead[j] - y * rows_of(x[k], j) for j in range(8)]
                for i in range(k + 1, 8):
                    x[i] = x[i] - low[i, k] * x[k]
        t_ref[base:base + 8, :] = jnp.where(lane <= base + sub, row * lax.rsqrt(piv_col), 0.0)
        if t == 15:
            break
        cols = ahead
        row = row * inv_col
        solved = [rows_of(row, k) for k in range(8)]
        for k in range(7, 0, -1):
            for j in range(k):
                solved[j] = solved[j] - low[k, j] * solved[k]
        for u in range(t + 1, 16):
            acc = jnp.where(inside, 0.0, tiles[u])
            for k in range(8):
                acc = acc - below[u - t - 1][k] * solved[k]
            tiles[u] = acc


def chol_kernel(counts_ref, g_ref, gt_ref, x_ref, o_ref, a_ref, tp_ref, t_ref, d_ref, acc_ref, xt_ref, tr_ref, vl_ref, vr_ref, z_ref):
    nb = 8
    size = 128 * nb
    for i in range(nb):
        for j in range(i + 1):
            m, o = (j, i - j) if i - j <= 4 else (i, 8 - i + j)
            for h in range(2):
                for p in range(8):
                    r = i * 128 + h * 64 + p * 8
                    a_ref[r:r + 8, j * 128:j * 128 + 128] = g_ref[h, p, m, o]
    for i in range(1, nb, 2):
        a_ref[128 * i - 128:128 * i, 128 * i:128 * i + 128] = jnp.zeros((128, 128), jnp.float32)
    z_ref[...] = jnp.zeros_like(z_ref)
    tr_ref[...] = jnp.zeros_like(tr_ref)
    tp_ref[...] = jnp.zeros_like(tp_ref)
    d_ref[...] = a_ref[:128, :128]

    def step(kb, carry):
        past = pl.multiple_of(jnp.maximum(kb - 1, 0) * 128, 128)
        here = pl.multiple_of(kb * 128, 128)
        col = a_ref[:, pl.ds(past, 128)]
        row_ids = lax.broadcasted_iota(jnp.int32, (size, 128), 0)
        mine = (row_ids >= here) & (kb > 0)
        v = jnp.where(mine, wide(left_terms(col), tr_ref[...]), 0.0)
        a_ref[:, pl.ds(past, 128)] = jnp.where(mine, v, col)
        vl_ref[...] = left_terms(v)
        vr_ref[...] = right_terms(v)
        for left in range(0, size, 256):
            part = wide(vl_ref[left:, :], vr_ref[left:left + 256, :])
            a_ref[left:, left:left + 256] = a_ref[left:, left:left + 256] - part
        factor_inverse(d_ref, t_ref, z_ref[...])
        tri = t_ref[...]
        half = pl.multiple_of((kb % 2) * 128, 128)
        tp_ref[kb // 2, pl.ds(half, 128), pl.ds(half, 128)] = tri
        right = right_terms(tri)
        tr_ref[...] = right
        then = pl.multiple_of(jnp.minimum(kb + 1, nb - 1) * 128, 128)
        v = wide(left_terms(a_ref[pl.ds(then, 128), pl.ds(here, 128)]), right)
        d_ref[...] = a_ref[pl.ds(then, 128), pl.ds(then, 128)] - wide(left_terms(v), right_terms(v))
        return carry

    lax.fori_loop(0, nb, step, 0)
    for q in range(nb // 2):
        s = 256 * q
        link = mm3(a_ref[s + 128:s + 256, s:s + 128], tp_ref[q, :128, :128], NN)
        tp_ref[q, 128:, :128] = -mm3(tp_ref[q, 128:, 128:], link, NN)
    acc_ref[...] = gt_ref[...]
    for q in range(nb // 2 - 1, -1, -1):
        s = slice(256 * q, 256 * q + 256)
        part = mm3(acc_ref[:, s], tp_ref[q], NN)
        xt_ref[:, s] = part
        if q:
            acc_ref[:, :256 * q] = acc_ref[:, :256 * q] - mm3(part, a_ref[s, :256 * q], NN)
    proj = mm3(xt_ref[...], x_ref[...], NT)
    _, count = own_rows(counts_ref, counts_ref.shape[1])
    slot = lax.broadcasted_iota(jnp.int32, o_ref.shape, 1)
    o_ref[...] = jnp.where(slot < count, jnp.sum(proj * proj, axis=0, keepdims=True), 0.0)


def chol_call(counts, g, gt, x):
    vm = pl.BlockSpec(memory_space=pltpu.VMEM)
    f32, bf16 = jnp.float32, jnp.bfloat16
    return pl.pallas_call(
        chol_kernel,
        out_shape=jax.ShapeDtypeStruct((1, 256), f32),
        in_specs=[pl.BlockSpec(memory_space=pltpu.SMEM)] + [vm] * 3, out_specs=vm,
        scratch_shapes=[pltpu.VMEM((1024, 1024), f32), pltpu.VMEM((4, 256, 256), f32), pltpu.VMEM((128, 128), f32),
                        pltpu.VMEM((128, 128), f32), pltpu.VMEM((64, 1024), f32), pltpu.VMEM((64, 1024), f32),
                        pltpu.VMEM((128, 768), bf16), pltpu.VMEM((1024, 768), bf16), pltpu.VMEM((1024, 768), bf16),
                        pltpu.VMEM((8, 128), f32)],
        compiler_params=pltpu.CompilerParams(vmem_limit_bytes=48 * 1024 * 1024),
    )(counts, g, gt, x)


def shards(matrix, counts, sign_bits, samples, gaussian):
    n_mix, n_dp = lax.axis_size("mix"), lax.axis_size("dp")
    grams = gram_call(n_mix, math.isqrt(n_dp), counts, samples, sign_bits[None, :], matrix)
    return chol_call(counts, grams, gaussian.T, matrix)[0]


def solution(mesh):
    in_specs = (P(("dp", "mix"), None), P("dp", None), P(("dp", "mix")), P("dp", None), P())
    out_specs = P(("dp", "mix"))
    return jax.shard_map(shards, mesh=mesh, in_specs=in_specs, out_specs=out_specs, check_vma=False)
```

```python
import functools
import math

import jax
import jax.numpy as jnp
from jax import lax
from jax.experimental import pallas as pl
from jax.experimental.pallas import tpu as pltpu
from jax.sharding import PartitionSpec as P

HI = lax.Precision.HIGHEST
NN = (((1,), (0,)), ((), ()))
NT = (((1,), (1,)), ((), ()))
TN = (((0,), (0,)), ((), ()))
MESH = pl.DeviceIdType.MESH
CHUNKS = 4


def own_rows(counts_ref, n_mix):
    m = lax.axis_index("mix")
    first, count = jnp.int32(0), jnp.int32(0)
    for i in range(n_mix):
        first = first + jnp.where(i < m, counts_ref[0, i], 0)
        count = count + jnp.where(i == m, counts_ref[0, i], 0)
    return first, count


def gram_kernel(n_mix, n, counts_ref, samples_ref, bits_ref, x_ref, g_ref,
                part, r1, s_all, w, r3, q, r4, f, *sems):
    (s1, v1, s2, v2, s3, v3, s4, v4, s5, v5, s6, v6, s7, v7, local) = sems
    dp, m = lax.axis_index("dp"), lax.axis_index("mix")
    y, z = dp // n, dp % n
    x, core = m // 2, m % 2
    nx = n_mix // 2
    n_off = n_mix // 2 + 1
    piece = 128 // (2 * n)
    capacity, picks = x_ref.shape[0], samples_ref.shape[1]

    def mix_peer(d):
        return (dp, (m + d) % n_mix)

    def y_peer(d):
        return (((y + d) % n) * n + z, m)

    def z_peer(d):
        return (y * n + (z + d) % n, m)

    barrier = pltpu.get_barrier_semaphore()
    for d in range(1, n_mix):
        pl.semaphore_signal(barrier, inc=1, device_id=mix_peer(d), device_id_type=MESH)
    for d in range(1, n):
        pl.semaphore_signal(barrier, inc=1, device_id=y_peer(d), device_id_type=MESH)
        pl.semaphore_signal(barrier, inc=1, device_id=z_peer(d), device_id_type=MESH)

    def send(src, dst, ssem, rsem, peer):
        copy = pltpu.make_async_remote_copy(src_ref=src, dst_ref=dst, send_sem=ssem, recv_sem=rsem,
                                            device_id=peer, device_id_type=MESH)
        copy.start()
        return copy

    first, count = own_rows(counts_ref, n_mix)
    slot = lax.broadcasted_iota(jnp.int32, (8, capacity), 1)
    row = lax.broadcasted_iota(jnp.int32, (8, capacity), 0)
    sign = jnp.where(slot < count, 2 * bits_ref[...] - 1, 0)
    table = []
    for base in range(0, picks, 8):
        sample = jnp.zeros((8, capacity), jnp.int32)
        for i in range(8):
            sample = jnp.where(row == i, samples_ref[0, base + i], sample)
        odd = jnp.bitwise_and(sample, first + slot)
        for shift in (8, 4, 2, 1):
            odd = jnp.bitwise_xor(odd, jnp.right_shift(odd, shift))
        table.append(jnp.where(jnp.bitwise_and(odd, 1) == 1, -sign, sign))
    table = jnp.concatenate(table, axis=0).astype(jnp.float32).astype(jnp.bfloat16)
    scale = 1.0 / math.sqrt(n_mix * 128 * picks)
    for b in range(n_mix):
        rest = x_ref[:, 128 * b:128 * b + 128]
        total = None
        for _ in range(3):
            term = rest.astype(jnp.bfloat16)
            rest = rest - term.astype(jnp.float32)
            product = lax.dot_general(table, term, NN, preferred_element_type=jnp.float32)
            total = product if total is None else total + product
        part[b] = total * scale
    pl.semaphore_wait(barrier, n_mix - 1 + 2 * (n - 1))
    sent = []

    got = []
    for d in range(1, n_mix):
        p = (m + d) % n_mix
        got.append(send(part.at[p], r1.at[m], s1.at[d], v1.at[d], mix_peer(d)))
    r1[m] = part[m]
    for copy in got:
        copy.wait_recv()
    sent += got
    s_all[m] = functools.reduce(jnp.add, [r1[b] for b in range(n_mix)])
    got = []
    for d in range(1, n_off):
        got.append(send(s_all.at[m], s_all.at[m], s2.at[d], v2.at[d], mix_peer(n_mix - d)))
    for copy in got:
        copy.wait_recv()
    sent += got

    for o in range(n_off):
        b = (m + o) % n_mix
        low, high = jnp.minimum(m, b), jnp.maximum(m, b)
        tile = lax.dot_general(s_all[high], s_all[low], TN, precision=HI, preferred_element_type=jnp.float32)
        for h in range(2):
            for p in range(n):
                r = (h * n + p) * piece
                w[h, p, o] = tile[r:r + piece]

    got = []
    for d in range(1, n):
        got.append(send(w.at[0, (y + d) % n], r3.at[0, y], s3.at[0, d], v3.at[0, d], y_peer(d)))
        got.append(send(w.at[1, (z + d) % n], r3.at[1, z], s3.at[1, d], v3.at[1, d], z_peer(d)))
    r3[0, y] = w[0, y]
    r3[1, z] = w[1, z]
    for copy in got:
        copy.wait_recv()
    sent += got
    for h in range(2):
        q[h] = functools.reduce(jnp.add, [r3[h, p] for p in range(n)])
    got = []
    for d in range(1, n):
        got.append(send(q.at[0], r4.at[0, z], s4.at[0, d], v4.at[0, d], z_peer(d)))
        got.append(send(q.at[1], r4.at[1, y], s4.at[1, d], v4.at[1, d], y_peer(d)))
    r4[0, z] = q[0]
    r4[1, y] = q[1]
    for copy in got:
        copy.wait_recv()
    sent += got
    for h in range(2):
        f[h, m] = functools.reduce(jnp.add, [r4[h, p] for p in range(n)])

    got = []
    for d in range(nx):
        column = ((x + d) % nx) * 2
        if d:
            got.append(send(f.at[core, m], f.at[core, m], s5.at[0, d], v5.at[0, d], (dp, column + core)))
        got.append(send(f.at[1 - core, m], f.at[1 - core, m], s5.at[1, d], v5.at[1, d], (dp, column + 1 - core)))
    for copy in got:
        copy.wait_recv()
    sent += got

    place = y + core * (z - y)
    sibling = (dp, m + 1 - 2 * core)
    up = (((y + 1 - core) % n) * n + (z + core) % n, m)
    down = (((y + n - 1 + core) % n) * n + (z + n - core) % n, m)
    width = n_mix // CHUNKS
    far = n // 2
    own = pltpu.make_async_copy(f.at[core], g_ref.at[core, place], local)
    own.start()

    def relay(way, d, c, source):
        at = (place + (n - d if way == 0 else d)) % n
        rows = pl.ds(c * width, width)
        dst = g_ref.at[core, at, rows]
        return send(source if d == 0 else dst, dst, s6.at[way, d, c], v6.at[way, d, c], (up, down)[way])

    def goes(way, d, c):
        return d < far - 1 or (d == far - 1 and (c < CHUNKS // 2) == (way == 0))

    moves = {}
    across = []
    for c in range(CHUNKS):
        for way in range(2):
            if goes(way, 0, c):
                moves[way, 0, c] = relay(way, 0, c, f.at[core, pl.ds(c * width, width)])
    across.append(send(f.at[core], g_ref.at[core, place], s7.at[0, 0, 0], v7.at[0, 0, 0], sibling))
    for d in range(1, far + 1):
        for c in range(CHUNKS):
            for way in range(2):
                if goes(way, d - 1, c):
                    moves[way, d - 1, c].wait_recv()
                    if goes(way, d, c):
                        moves[way, d, c] = relay(way, d, c, None)
                    at = (place + (n - d if way == 0 else d)) % n
                    block = g_ref.at[core, at, pl.ds(c * width, width)]
                    across.append(send(block, block, s7.at[way, d, c], v7.at[way, d, c], sibling))
    own.wait()
    for copy in across:
        copy.wait_recv()
    for copy in sent + across + list(moves.values()):
        copy.wait_send()


def mm(a, b, dims):
    return lax.dot_general(a, b, dims, precision=HI, preferred_element_type=jnp.float32)


def split(x):
    high = x.astype(jnp.bfloat16)
    rest = x - high.astype(jnp.float32)
    mid = rest.astype(jnp.bfloat16)
    return high, mid, (rest - mid.astype(jnp.float32)).astype(jnp.bfloat16)


def left_terms(x):
    high, mid, low = split(x)
    return jnp.concatenate([high, high, mid, high, low, mid], axis=1)


def right_terms(x):
    high, mid, low = split(x)
    return jnp.concatenate([high, mid, high, low, high, mid], axis=1)


def wide(a, b):
    return lax.dot_general(a, b, NT, preferred_element_type=jnp.float32)


def mm3(a, b, dims):
    ah, bh = a.astype(jnp.bfloat16), b.astype(jnp.bfloat16)
    al = (a - ah.astype(jnp.float32)).astype(jnp.bfloat16)
    bl = (b - bh.astype(jnp.float32)).astype(jnp.bfloat16)
    dot = functools.partial(lax.dot_general, dimension_numbers=dims, preferred_element_type=jnp.float32)
    return dot(ah, bh) + (dot(ah, bl) + dot(al, bh))


def factor_inverse(d_ref, t_ref, zero):
    shape = (8, 128)
    lane = lax.broadcasted_iota(jnp.int32, shape, 1)
    sub = lax.broadcasted_iota(jnp.int32, shape, 0)
    tiles = [d_ref[8 * t:8 * t + 8, :] for t in range(16)]
    lanes_of = lambda x, c: jnp.broadcast_to(x[:, c:c + 1], shape)
    rows_of = lambda x, r: jnp.broadcast_to(x[r:r + 1, :], shape)
    cols = [lanes_of(tiles[0], j) + zero for j in range(8)]
    for t in range(16):
        base = 8 * t
        inside = (lane >= base) & (lane < base + 8)
        below = [[lanes_of(tiles[u], base + j) for j in range(8)] for u in range(t + 1, 16)]
        if t < 15:
            x = [b + zero for b in below[0]]
            ahead = [lanes_of(tiles[t + 1], base + 8 + j) + zero for j in range(8)]
        row = jnp.where(inside, jnp.where(lane == base + sub, 1.0, 0.0), tiles[t])
        low, inv_col, piv_col = {}, zero, zero + 1.0
        for k in range(8):
            pivot = rows_of(cols[k], k)
            inv = 1.0 / pivot
            factor = cols[k] * inv
            for j in range(k + 1, 8):
                cols[j] = cols[j] - factor * rows_of(cols[k], j)
                low[j, k] = rows_of(factor, j)
            inv_col = jnp.where(sub == k, inv, inv_col)
            piv_col = jnp.where(sub == k, pivot, piv_col)
            if k < 7:
                row = row - jnp.where(sub > k, factor, 0.0) * rows_of(row, k)
            if t < 15:
                y = x[k] * inv
                ahead = [ahead[j] - y * rows_of(x[k], j) for j in range(8)]
                for i in range(k + 1, 8):
                    x[i] = x[i] - low[i, k] * x[k]
        t_ref[base:base + 8, :] = jnp.where(lane <= base + sub, row * lax.rsqrt(piv_col), 0.0)
        if t == 15:
            break
        cols = ahead
        row = row * inv_col
        solved = [rows_of(row, k) for k in range(8)]
        for k in range(7, 0, -1):
            for j in range(k):
                solved[j] = solved[j] - low[k, j] * solved[k]
        for u in range(t + 1, 16):
            acc = jnp.where(inside, 0.0, tiles[u])
            for k in range(8):
                acc = acc - below[u - t - 1][k] * solved[k]
            tiles[u] = acc


def chol_kernel(counts_ref, g_ref, gt_ref, x_ref, o_ref, a_ref, tp_ref, t_ref, d_ref, acc_ref, xt_ref, tr_ref, vl_ref, vr_ref, z_ref):
    nb = 8
    size = 128 * nb
    for i in range(nb):
        for j in range(i + 1):
            m, o = (j, i - j) if i - j <= 4 else (i, 8 - i + j)
            for h in range(2):
                for p in range(8):
                    r = i * 128 + h * 64 + p * 8
                    a_ref[r:r + 8, j * 128:j * 128 + 128] = g_ref[h, p, m, o]
    for i in range(1, nb, 2):
        a_ref[128 * i - 128:128 * i, 128 * i:128 * i + 128] = jnp.zeros((128, 128), jnp.float32)
    z_ref[...] = jnp.zeros_like(z_ref)
    tr_ref[...] = jnp.zeros_like(tr_ref)
    tp_ref[...] = jnp.zeros_like(tp_ref)
    d_ref[...] = a_ref[:128, :128]

    def step(kb, carry):
        past = pl.multiple_of(jnp.maximum(kb - 1, 0) * 128, 128)
        here = pl.multiple_of(kb * 128, 128)
        col = a_ref[:, pl.ds(past, 128)]
        row_ids = lax.broadcasted_iota(jnp.int32, (size, 128), 0)
        mine = (row_ids >= here) & (kb > 0)
        v = jnp.where(mine, wide(left_terms(col), tr_ref[...]), 0.0)
        a_ref[:, pl.ds(past, 128)] = jnp.where(mine, v, col)
        vl_ref[...] = left_terms(v)
        vr_ref[...] = right_terms(v)
        for left in range(0, size, 256):
            part = wide(vl_ref[left:, :], vr_ref[left:left + 256, :])
            a_ref[left:, left:left + 256] = a_ref[left:, left:left + 256] - part
        factor_inverse(d_ref, t_ref, z_ref[...])
        tri = t_ref[...]
        half = pl.multiple_of((kb % 2) * 128, 128)
        tp_ref[kb // 2, pl.ds(half, 128), pl.ds(half, 128)] = tri
        right = right_terms(tri)
        tr_ref[...] = right
        then = pl.multiple_of(jnp.minimum(kb + 1, nb - 1) * 128, 128)
        v = wide(left_terms(a_ref[pl.ds(then, 128), pl.ds(here, 128)]), right)
        d_ref[...] = a_ref[pl.ds(then, 128), pl.ds(then, 128)] - wide(left_terms(v), right_terms(v))
        return carry

    lax.fori_loop(0, nb, step, 0)
    for q in range(nb // 2):
        s = 256 * q
        link = mm3(a_ref[s + 128:s + 256, s:s + 128], tp_ref[q, :128, :128], NN)
        tp_ref[q, 128:, :128] = -mm3(tp_ref[q, 128:, 128:], link, NN)
    acc_ref[...] = gt_ref[...]
    for q in range(nb // 2 - 1, -1, -1):
        s = slice(256 * q, 256 * q + 256)
        part = mm3(acc_ref[:, s], tp_ref[q], NN)
        xt_ref[:, s] = part
        if q:
            acc_ref[:, :256 * q] = acc_ref[:, :256 * q] - mm3(part, a_ref[s, :256 * q], NN)
    proj = mm3(xt_ref[...], x_ref[...], NT)
    _, count = own_rows(counts_ref, counts_ref.shape[1])
    slot = lax.broadcasted_iota(jnp.int32, o_ref.shape, 1)
    o_ref[...] = jnp.where(slot < count, jnp.sum(proj * proj, axis=0, keepdims=True), 0.0)


def fused_kernel(n_mix, n, counts_ref, samples_ref, bits_ref, x_ref, gt_ref, o_ref, g_ref, *scratch):
    gram_kernel(n_mix, n, counts_ref, samples_ref, bits_ref, x_ref, g_ref, *scratch[:-10])
    chol_kernel(counts_ref, g_ref, gt_ref, x_ref, o_ref, *scratch[-10:])


def fused_call(n_mix, n, counts, samples, bits, x, gt):
    vm = pl.BlockSpec(memory_space=pltpu.VMEM)
    sm = pl.BlockSpec(memory_space=pltpu.SMEM)
    n_off, piece, k = n_mix // 2 + 1, 128 // (2 * n), samples.shape[1]
    f32, bf16 = jnp.float32, jnp.bfloat16
    dma = pltpu.SemaphoreType.DMA
    pair = lambda *s: [dma(s), dma(s)]
    return pl.pallas_call(
        functools.partial(fused_kernel, n_mix, n),
        out_shape=jax.ShapeDtypeStruct((1, 256), f32),
        in_specs=[sm, sm, vm, vm, vm], out_specs=vm,
        scratch_shapes=[
            pltpu.VMEM((2, n, n_mix, n_off, piece, 128), f32),
            pltpu.VMEM((n_mix, k, 128), f32), pltpu.VMEM((n_mix, k, 128), f32), pltpu.VMEM((n_mix, k, 128), f32),
            pltpu.VMEM((2, n, n_off, piece, 128), f32), pltpu.VMEM((2, n, n_off, piece, 128), f32),
            pltpu.VMEM((2, n_off, piece, 128), f32), pltpu.VMEM((2, n, n_off, piece, 128), f32),
            pltpu.VMEM((2, n_mix, n_off, piece, 128), f32),
            *pair(n_mix), *pair(n_mix), *pair(2, n), *pair(2, n), *pair(2, n_mix // 2),
            *pair(2, n // 2 + 1, CHUNKS), *pair(2, n // 2 + 1, CHUNKS), dma(()),
            pltpu.VMEM((1024, 1024), f32), pltpu.VMEM((4, 256, 256), f32), pltpu.VMEM((128, 128), f32),
            pltpu.VMEM((128, 128), f32), pltpu.VMEM((64, 1024), f32), pltpu.VMEM((64, 1024), f32),
            pltpu.VMEM((128, 768), bf16), pltpu.VMEM((1024, 768), bf16), pltpu.VMEM((1024, 768), bf16),
            pltpu.VMEM((8, 128), f32)],
        compiler_params=pltpu.CompilerParams(collective_id=0, has_side_effects=True, vmem_limit_bytes=48 * 1024 * 1024),
    )(counts, samples, bits, x, gt)


def shards(matrix, counts, sign_bits, samples, gaussian):
    n_mix, n_dp = lax.axis_size("mix"), lax.axis_size("dp")
    return fused_call(n_mix, math.isqrt(n_dp), counts, samples, sign_bits[None, :], matrix, gaussian.T)[0]


def solution(mesh):
    in_specs = (P(("dp", "mix"), None), P("dp", None), P(("dp", "mix")), P("dp", None), P())
    out_specs = P(("dp", "mix"))
    return jax.shard_map(shards, mesh=mesh, in_specs=in_specs, out_specs=out_specs, check_vma=False)
```

```python
import functools
import math

import jax
import jax.numpy as jnp
from jax import lax
from jax.experimental import pallas as pl
from jax.experimental.pallas import tpu as pltpu
from jax.sharding import PartitionSpec as P

HI = lax.Precision.HIGHEST
NN = (((1,), (0,)), ((), ()))
NT = (((1,), (1,)), ((), ()))
TN = (((0,), (0,)), ((), ()))
MESH = pl.DeviceIdType.MESH
TILES = [(i, j) for j in range(8) for i in range(j, 8)]
SLOTS = 5
WAVES = ((0, 1), (1, 4))
PASSES = ((0, 1), (1, 1), (2, 1), (3, 2))


def own_rows(counts_ref, n_mix):
    m = lax.axis_index("mix")
    first, count = jnp.int32(0), jnp.int32(0)
    for i in range(n_mix):
        first = first + jnp.where(i < m, counts_ref[0, i], 0)
        count = count + jnp.where(i == m, counts_ref[0, i], 0)
    return first, count


def mm(a, b, dims):
    return lax.dot_general(a, b, dims, precision=HI, preferred_element_type=jnp.float32)


def split(x):
    high = x.astype(jnp.bfloat16)
    rest = x - high.astype(jnp.float32)
    mid = rest.astype(jnp.bfloat16)
    return high, mid, (rest - mid.astype(jnp.float32)).astype(jnp.bfloat16)


def left_terms(x):
    high, mid, low = split(x)
    return jnp.concatenate([high, high, mid, high, low, mid], axis=1)


def right_terms(x):
    high, mid, low = split(x)
    return jnp.concatenate([high, mid, high, low, high, mid], axis=1)


def wide(a, b):
    return lax.dot_general(a, b, NT, preferred_element_type=jnp.float32)


def mm3(a, b, dims):
    ah, bh = a.astype(jnp.bfloat16), b.astype(jnp.bfloat16)
    al = (a - ah.astype(jnp.float32)).astype(jnp.bfloat16)
    bl = (b - bh.astype(jnp.float32)).astype(jnp.bfloat16)
    dot = functools.partial(lax.dot_general, dimension_numbers=dims, preferred_element_type=jnp.float32)
    return dot(ah, bh) + (dot(ah, bl) + dot(al, bh))


def factor_inverse(d_ref, t_ref, zero):
    shape = (8, 128)
    lane = lax.broadcasted_iota(jnp.int32, shape, 1)
    sub = lax.broadcasted_iota(jnp.int32, shape, 0)
    tiles = [d_ref[8 * t:8 * t + 8, :] for t in range(16)]
    lanes_of = lambda x, c: jnp.broadcast_to(x[:, c:c + 1], shape)
    rows_of = lambda x, r: jnp.broadcast_to(x[r:r + 1, :], shape)
    cols = [lanes_of(tiles[0], j) + zero for j in range(8)]
    for t in range(16):
        base = 8 * t
        inside = (lane >= base) & (lane < base + 8)
        below = [[lanes_of(tiles[u], base + j) for j in range(8)] for u in range(t + 1, 16)]
        if t < 15:
            x = [b + zero for b in below[0]]
            ahead = [lanes_of(tiles[t + 1], base + 8 + j) + zero for j in range(8)]
        row = jnp.where(inside, jnp.where(lane == base + sub, 1.0, 0.0), tiles[t])
        low, inv_col, piv_col = {}, zero, zero + 1.0
        for k in range(8):
            pivot = rows_of(cols[k], k)
            inv = 1.0 / pivot
            factor = cols[k] * inv
            for j in range(k + 1, 8):
                cols[j] = cols[j] - factor * rows_of(cols[k], j)
                low[j, k] = rows_of(factor, j)
            inv_col = jnp.where(sub == k, inv, inv_col)
            piv_col = jnp.where(sub == k, pivot, piv_col)
            if k < 7:
                row = row - jnp.where(sub > k, factor, 0.0) * rows_of(row, k)
            if t < 15:
                y = x[k] * inv
                ahead = [ahead[j] - y * rows_of(x[k], j) for j in range(8)]
                for i in range(k + 1, 8):
                    x[i] = x[i] - low[i, k] * x[k]
        t_ref[base:base + 8, :] = jnp.where(lane <= base + sub, row * lax.rsqrt(piv_col), 0.0)
        if t == 15:
            break
        cols = ahead
        row = row * inv_col
        solved = [rows_of(row, k) for k in range(8)]
        for k in range(7, 0, -1):
            for j in range(k):
                solved[j] = solved[j] - low[k, j] * solved[k]
        for u in range(t + 1, 16):
            acc = jnp.where(inside, 0.0, tiles[u])
            for k in range(8):
                acc = acc - below[u - t - 1][k] * solved[k]
            tiles[u] = acc


def is_equal(a, b):
    return 1 - jnp.minimum(1, jnp.maximum(a - b, b - a))


def fused_kernel(n_mix, n, counts_ref, samples_ref, bits_ref, x_ref, gt_ref, o_ref, g_ref,
                 part, r1, s_all, w0, w1, r30, r31, q0, q1, r40, r41, f0, f1, *rest):
    (s1, v1, s2, v2, s3, v3, s4, v4, s5, v5, s6, v6, s7, v7, local,
     a_ref, tp_ref, t_ref, d_ref, acc_ref, xt_ref, tr_ref, vl_ref, vr_ref, z_ref) = rest
    w, r3, q, r4, f = (w0, w1), (r30, r31), (q0, q1), (r40, r41), (f0, f1)
    dp, m = lax.axis_index("dp"), lax.axis_index("mix")
    y, z = dp // n, dp % n
    x, core = m // 2, m % 2
    nx = n_mix // 2
    nb = n_mix
    size = 128 * nb
    piece = 128 // (2 * n)
    capacity, picks = x_ref.shape[0], samples_ref.shape[1]

    def mix_peer(d):
        return (dp, (m + d) % n_mix)

    def y_peer(d):
        return (((y + d) % n) * n + z, m)

    def z_peer(d):
        return (y * n + (z + d) % n, m)

    barrier = pltpu.get_barrier_semaphore()
    for d in range(1, n_mix):
        pl.semaphore_signal(barrier, inc=1, device_id=mix_peer(d), device_id_type=MESH)
    for d in range(1, n):
        pl.semaphore_signal(barrier, inc=1, device_id=y_peer(d), device_id_type=MESH)
        pl.semaphore_signal(barrier, inc=1, device_id=z_peer(d), device_id_type=MESH)

    def remote(src, dst, ssem, rsem, peer):
        return pltpu.make_async_remote_copy(src_ref=src, dst_ref=dst, send_sem=ssem, recv_sem=rsem,
                                            device_id=peer, device_id_type=MESH)

    sent = []

    def send(*what):
        copy = remote(*what)
        copy.start()
        sent.append(copy)
        return copy

    def received(copies):
        for copy in copies:
            copy.wait_recv()

    first, count = own_rows(counts_ref, n_mix)
    slot = lax.broadcasted_iota(jnp.int32, (8, capacity), 1)
    row = lax.broadcasted_iota(jnp.int32, (8, capacity), 0)
    sign = jnp.where(slot < count, 2 * bits_ref[...] - 1, 0)
    table = []
    for base in range(0, picks, 8):
        sample = jnp.zeros((8, capacity), jnp.int32)
        for i in range(8):
            sample = jnp.where(row == i, samples_ref[0, base + i], sample)
        odd = jnp.bitwise_and(sample, first + slot)
        for shift in (8, 4, 2, 1):
            odd = jnp.bitwise_xor(odd, jnp.right_shift(odd, shift))
        table.append(jnp.where(jnp.bitwise_and(odd, 1) == 1, -sign, sign))
    table = jnp.concatenate(table, axis=0).astype(jnp.float32).astype(jnp.bfloat16)
    scale = 1.0 / math.sqrt(n_mix * 128 * picks)
    for b in range(n_mix):
        rest_of = x_ref[:, 128 * b:128 * b + 128]
        total = None
        for _ in range(3):
            term = rest_of.astype(jnp.bfloat16)
            rest_of = rest_of - term.astype(jnp.float32)
            product = lax.dot_general(table, term, NN, preferred_element_type=jnp.float32)
            total = product if total is None else total + product
        part[b] = total * scale
    pl.semaphore_wait(barrier, n_mix - 1 + 2 * (n - 1))

    got = []
    for d in range(1, n_mix):
        p = (m + d) % n_mix
        got.append(send(part.at[p], r1.at[m], s1.at[d], v1.at[d], mix_peer(d)))
    r1[m] = part[m]
    a_ref[...] = jnp.zeros_like(a_ref)
    tp_ref[...] = jnp.zeros_like(tp_ref)
    tr_ref[...] = jnp.zeros_like(tr_ref)
    z_ref[...] = jnp.zeros_like(z_ref)
    received(got)
    s_all[m] = functools.reduce(jnp.add, [r1[b] for b in range(n_mix)])
    received([send(s_all.at[m], s_all.at[m], s2.at[d], v2.at[d], mix_peer(d)) for d in range(1, n_mix)])

    def tiles(k):
        start, many = WAVES[k]
        for s in range(start, start + many):
            own = [TILES[min(n_mix * s + b, len(TILES) - 1)] for b in range(n_mix)]
            i = sum(own[b][0] * is_equal(m, b) for b in range(n_mix))
            j = sum(own[b][1] * is_equal(m, b) for b in range(n_mix))
            tile = lax.dot_general(s_all[i], s_all[j], TN, precision=HI, preferred_element_type=jnp.float32)
            for h in range(2):
                for p in range(n):
                    r = (h * n + p) * piece
                    w[k][h, p, s - start] = tile[r:r + piece]

    def reduce_first(k):
        got = []
        for d in range(1, n):
            got.append(send(w[k].at[0, (y + d) % n], r3[k].at[0, y], s3.at[k, 0, d], v3.at[k, 0, d], y_peer(d)))
            got.append(send(w[k].at[1, (z + d) % n], r3[k].at[1, z], s3.at[k, 1, d], v3.at[k, 1, d], z_peer(d)))
        r3[k][0, y] = w[k][0, y]
        r3[k][1, z] = w[k][1, z]
        return got

    def reduce_second(k, got):
        received(got)
        for h in range(2):
            q[k][h] = functools.reduce(jnp.add, [r3[k][h, p] for p in range(n)])
        got = []
        for d in range(1, n):
            got.append(send(q[k].at[0], r4[k].at[0, z], s4.at[k, 0, d], v4.at[k, 0, d], z_peer(d)))
            got.append(send(q[k].at[1], r4[k].at[1, y], s4.at[k, 1, d], v4.at[k, 1, d], y_peer(d)))
        r4[k][0, z] = q[k][0]
        r4[k][1, y] = q[k][1]
        return got

    def gather_mix(k, got):
        received(got)
        for h in range(2):
            f[k][h, m] = functools.reduce(jnp.add, [r4[k][h, p] for p in range(n)])
        got = []
        for d in range(nx):
            column = ((x + d) % nx) * 2
            if d:
                got.append(send(f[k].at[core, m], f[k].at[core, m], s5.at[k, 0, d], v5.at[k, 0, d], (dp, column + core)))
            got.append(send(f[k].at[1 - core, m], f[k].at[1 - core, m], s5.at[k, 1, d], v5.at[k, 1, d], (dp, column + 1 - core)))
        return got

    place = y + core * (z - y)
    sibling = (dp, m + 1 - 2 * core)

    def source(k):
        start, many = PASSES[k]
        return f0.at[core] if k == 0 else f1.at[core, :, pl.ds(start - 1, many)]

    def block(k, d):
        start, many = PASSES[k]
        return g_ref.at[core, (place + n - d) % n, :, pl.ds(start, many)]

    def place_copy(k, d):
        peer = (((y + d * (1 - core)) % n) * n + (z + d * core) % n, m)
        return remote(source(k), block(k, 0), s6.at[k, d], v6.at[k, d], peer)

    def own_copy(k):
        return pltpu.make_async_copy(source(k), block(k, 0), local.at[k])

    def core_copy(k, d):
        return remote(block(k, d) if d else source(k), block(k, d), s7.at[k, d], v7.at[k, d], sibling)

    def gather_places(k):
        for d in range(1, n):
            place_copy(k, d).start()
        core_copy(k, 0).start()
        own_copy(k).start()

    def pass_on(k):
        for d in range(1, n):
            place_copy(k, d).wait_recv()
            core_copy(k, d).start()

    def absorb(k):
        own_copy(k).wait()
        for d in range(n):
            core_copy(k, d).wait_recv()
        start, many = PASSES[k]
        for s in range(start, start + many):
            for b in range(n_mix):
                if n_mix * s + b < len(TILES):
                    i, j = TILES[n_mix * s + b]
                    for h in range(2):
                        for p in range(n):
                            r = i * 128 + (h * n + p) * piece
                            a_ref[r:r + piece, 128 * j:128 * j + 128] = a_ref[r:r + piece, 128 * j:128 * j + 128] + g_ref[h, p, b, s]

    tiles(0)
    early = reduce_first(0)
    tiles(1)
    late = reduce_first(1)
    early = reduce_second(0, early)
    late = reduce_second(1, late)
    early = gather_mix(0, early)
    received(early)
    gather_places(0)
    late = gather_mix(1, late)
    received(late)
    for k in range(1, len(PASSES)):
        gather_places(k)
    pass_on(0)
    absorb(0)
    d_ref[...] = a_ref[:128, :128]

    def step(kb, carry):
        past = pl.multiple_of(jnp.maximum(kb - 1, 0) * 128, 128)
        here = pl.multiple_of(kb * 128, 128)
        col = a_ref[:, pl.ds(past, 128)]
        row_ids = lax.broadcasted_iota(jnp.int32, (size, 128), 0)
        mine = (row_ids >= here) & (kb > 0)
        v = jnp.where(mine, wide(left_terms(col), tr_ref[...]), 0.0)
        a_ref[:, pl.ds(past, 128)] = jnp.where(mine, v, col)
        vl_ref[...] = left_terms(v)
        vr_ref[...] = right_terms(v)
        for left in range(0, size, 256):
            update = wide(vl_ref[left:, :], vr_ref[left:left + 256, :])
            a_ref[left:, left:left + 256] = a_ref[left:, left:left + 256] - update
        factor_inverse(d_ref, t_ref, z_ref[...])
        tri = t_ref[...]
        half = pl.multiple_of((kb % 2) * 128, 128)
        tp_ref[kb // 2, pl.ds(half, 128), pl.ds(half, 128)] = tri
        tr_ref[...] = right_terms(tri)

        return carry

    def next_block(kb, carry):
        here = pl.multiple_of(kb * 128, 128)
        then = pl.multiple_of(jnp.minimum(kb + 1, nb - 1) * 128, 128)
        v = wide(left_terms(a_ref[pl.ds(then, 128), pl.ds(here, 128)]), tr_ref[...])
        d_ref[...] = a_ref[pl.ds(then, 128), pl.ds(then, 128)] - wide(left_terms(v), right_terms(v))
        return carry

    for kb in range(3):
        lax.fori_loop(kb, kb + 1, step, 0)
        pass_on(kb + 1)
        if kb == 0:
            absorb(1)
        if kb == 2:
            absorb(2)
        next_block(kb, 0)
    lax.fori_loop(3, 4, step, 0)
    absorb(3)
    next_block(3, 0)
    lax.fori_loop(4, nb, lambda kb, carry: next_block(kb, step(kb, carry)), 0)
    for p in range(nb // 2):
        s = 256 * p
        link = mm3(a_ref[s + 128:s + 256, s:s + 128], tp_ref[p, :128, :128], NN)
        tp_ref[p, 128:, :128] = -mm3(tp_ref[p, 128:, 128:], link, NN)
    acc_ref[...] = gt_ref[...]
    for p in range(nb // 2 - 1, -1, -1):
        s = slice(256 * p, 256 * p + 256)
        solved = mm3(acc_ref[:, s], tp_ref[p], NN)
        xt_ref[:, s] = solved
        if p:
            acc_ref[:, :256 * p] = acc_ref[:, :256 * p] - mm3(solved, a_ref[s, :256 * p], NN)
    proj = mm3(xt_ref[...], x_ref[...], NT)
    slot = lax.broadcasted_iota(jnp.int32, o_ref.shape, 1)
    o_ref[...] = jnp.where(slot < count, jnp.sum(proj * proj, axis=0, keepdims=True), 0.0)
    for copy in sent:
        copy.wait_send()
    for k in range(len(PASSES)):
        for d in range(n):
            if d:
                place_copy(k, d).wait_send()
            core_copy(k, d).wait_send()


def fused_call(n_mix, n, counts, samples, bits, x, gt):
    vm = pl.BlockSpec(memory_space=pltpu.VMEM)
    sm = pl.BlockSpec(memory_space=pltpu.SMEM)
    piece, k = 128 // (2 * n), samples.shape[1]
    f32, bf16 = jnp.float32, jnp.bfloat16
    dma = pltpu.SemaphoreType.DMA
    pair = lambda *s: [dma(s), dma(s)]
    waves = lambda *s: [pltpu.VMEM((*s, many, piece, 128), f32) for _, many in WAVES]
    return pl.pallas_call(
        functools.partial(fused_kernel, n_mix, n),
        out_shape=jax.ShapeDtypeStruct((1, x.shape[0]), f32),
        in_specs=[sm, sm, vm, vm, vm], out_specs=vm,
        scratch_shapes=[
            pltpu.VMEM((2, n, n_mix, SLOTS, piece, 128), f32),
            pltpu.VMEM((n_mix, k, 128), f32), pltpu.VMEM((n_mix, k, 128), f32), pltpu.VMEM((n_mix, k, 128), f32),
            *waves(2, n), *waves(2, n), *waves(2), *waves(2, n), *waves(2, n_mix),
            *pair(n_mix), *pair(n_mix), *pair(2, 2, n), *pair(2, 2, n), *pair(2, 2, n_mix // 2),
            *pair(len(PASSES), n), *pair(len(PASSES), n), dma((len(PASSES),)),
            pltpu.VMEM((1024, 1024), f32), pltpu.VMEM((4, 256, 256), f32), pltpu.VMEM((128, 128), f32),
            pltpu.VMEM((128, 128), f32), pltpu.VMEM((64, 1024), f32), pltpu.VMEM((64, 1024), f32),
            pltpu.VMEM((128, 768), bf16), pltpu.VMEM((1024, 768), bf16), pltpu.VMEM((1024, 768), bf16),
            pltpu.VMEM((8, 128), f32)],
        compiler_params=pltpu.CompilerParams(collective_id=0, has_side_effects=True, vmem_limit_bytes=48 * 1024 * 1024),
    )(counts, samples, bits, x, gt)


def shards(matrix, counts, sign_bits, samples, gaussian):
    n_mix, n_dp = lax.axis_size("mix"), lax.axis_size("dp")
    return fused_call(n_mix, math.isqrt(n_dp), counts, samples, sign_bits[None, :], matrix, gaussian.T)[0]


def solution(mesh):
    in_specs = (P(("dp", "mix"), None), P("dp", None), P(("dp", "mix")), P("dp", None), P())
    out_specs = P(("dp", "mix"))
    return jax.shard_map(shards, mesh=mesh, in_specs=in_specs, out_specs=out_specs, check_vma=False)
```

```python
import functools
import math

import jax
import jax.numpy as jnp
from jax import lax
from jax.experimental import pallas as pl
from jax.experimental.pallas import tpu as pltpu
from jax.sharding import PartitionSpec as P

HI = lax.Precision.HIGHEST
NN = (((1,), (0,)), ((), ()))
NT = (((1,), (1,)), ((), ()))
TN = (((0,), (0,)), ((), ()))
MESH = pl.DeviceIdType.MESH
TILES = [(i, j) for j in range(8) for i in range(j, 8)]
SLOTS = 5
WAVES = ((0, 1), (1, 4))
PASSES = ((0, 1), (1, 1), (2, 1), (3, 2))


def own_rows(counts_ref, n_mix):
    m = lax.axis_index("mix")
    first, count = jnp.int32(0), jnp.int32(0)
    for i in range(n_mix):
        first = first + jnp.where(i < m, counts_ref[0, i], 0)
        count = count + jnp.where(i == m, counts_ref[0, i], 0)
    return first, count


def mm(a, b, dims):
    return lax.dot_general(a, b, dims, precision=HI, preferred_element_type=jnp.float32)


def split(x):
    high = x.astype(jnp.bfloat16)
    rest = x - high.astype(jnp.float32)
    mid = rest.astype(jnp.bfloat16)
    return high, mid, (rest - mid.astype(jnp.float32)).astype(jnp.bfloat16)


def left_terms(x):
    high, mid, low = split(x)
    return jnp.concatenate([high, high, mid, high, low, mid], axis=1)


def right_terms(x):
    high, mid, low = split(x)
    return jnp.concatenate([high, mid, high, low, high, mid], axis=1)


def wide(a, b):
    return lax.dot_general(a, b, NT, preferred_element_type=jnp.float32)


def mm3(a, b, dims):
    ah, bh = a.astype(jnp.bfloat16), b.astype(jnp.bfloat16)
    al = (a - ah.astype(jnp.float32)).astype(jnp.bfloat16)
    bl = (b - bh.astype(jnp.float32)).astype(jnp.bfloat16)
    dot = functools.partial(lax.dot_general, dimension_numbers=dims, preferred_element_type=jnp.float32)
    return dot(ah, bh) + (dot(ah, bl) + dot(al, bh))


def factor_inverse(d_ref, t_ref, zero):
    shape = (8, 128)
    lane = lax.broadcasted_iota(jnp.int32, shape, 1)
    sub = lax.broadcasted_iota(jnp.int32, shape, 0)
    tiles = [d_ref[8 * t:8 * t + 8, :] for t in range(16)]
    lanes_of = lambda x, c: jnp.broadcast_to(x[:, c:c + 1], shape)
    rows_of = lambda x, r: jnp.broadcast_to(x[r:r + 1, :], shape)
    cols = [lanes_of(tiles[0], j) + zero for j in range(8)]
    for t in range(16):
        base = 8 * t
        inside = (lane >= base) & (lane < base + 8)
        below = [[lanes_of(tiles[u], base + j) for j in range(8)] for u in range(t + 1, 16)]
        if t < 15:
            x = [b + zero for b in below[0]]
            ahead = [lanes_of(tiles[t + 1], base + 8 + j) + zero for j in range(8)]
        row = jnp.where(inside, jnp.where(lane == base + sub, 1.0, 0.0), tiles[t])
        low, inv_col, piv_col = {}, zero, zero + 1.0
        for k in range(8):
            pivot = rows_of(cols[k], k)
            inv = 1.0 / pivot
            factor = cols[k] * inv
            for j in range(k + 1, 8):
                cols[j] = cols[j] - factor * rows_of(cols[k], j)
                low[j, k] = rows_of(factor, j)
            inv_col = jnp.where(sub == k, inv, inv_col)
            piv_col = jnp.where(sub == k, pivot, piv_col)
            if k < 7:
                row = row - jnp.where(sub > k, factor, 0.0) * rows_of(row, k)
            if t < 15:
                y = x[k] * inv
                ahead = [ahead[j] - y * rows_of(x[k], j) for j in range(8)]
                for i in range(k + 1, 8):
                    x[i] = x[i] - low[i, k] * x[k]
        t_ref[base:base + 8, :] = jnp.where(lane <= base + sub, row * lax.rsqrt(piv_col), 0.0)
        if t == 15:
            break
        cols = ahead
        row = row * inv_col
        solved = [rows_of(row, k) for k in range(8)]
        for k in range(7, 0, -1):
            for j in range(k):
                solved[j] = solved[j] - low[k, j] * solved[k]
        for u in range(t + 1, 16):
            acc = jnp.where(inside, 0.0, tiles[u])
            for k in range(8):
                acc = acc - below[u - t - 1][k] * solved[k]
            tiles[u] = acc


def is_equal(a, b):
    return 1 - jnp.minimum(1, jnp.maximum(a - b, b - a))


def fused_kernel(n_mix, n, counts_ref, samples_ref, bits_ref, x_ref, gt_ref, o_ref, g_ref,
                 part, r1, s_all, w0, w1, r30, r31, q0, q1, r40, r41, f0, f1, *rest):
    (s1, v1, s2, v2, s3, v3, s4, v4, s5, v5, s6, v6, s7, v7, local,
     a_ref, tp_ref, t_ref, d_ref, acc_ref, xt_ref, tr_ref, vl_ref, vr_ref, z_ref) = rest
    w, r3, q, r4, f = (w0, w1), (r30, r31), (q0, q1), (r40, r41), (f0, f1)
    dp, m = lax.axis_index("dp"), lax.axis_index("mix")
    y, z = dp // n, dp % n
    x, core = m // 2, m % 2
    nx = n_mix // 2
    nb = n_mix
    size = 128 * nb
    piece = 128 // (2 * n)
    capacity, picks = x_ref.shape[0], samples_ref.shape[1]

    def mix_peer(d):
        return (dp, (m + d) % n_mix)

    def y_peer(d):
        return (((y + d) % n) * n + z, m)

    def z_peer(d):
        return (y * n + (z + d) % n, m)

    barrier = pltpu.get_barrier_semaphore()
    for d in range(1, n_mix):
        pl.semaphore_signal(barrier, inc=1, device_id=mix_peer(d), device_id_type=MESH)
    for d in range(1, n):
        pl.semaphore_signal(barrier, inc=1, device_id=y_peer(d), device_id_type=MESH)
        pl.semaphore_signal(barrier, inc=1, device_id=z_peer(d), device_id_type=MESH)

    def remote(src, dst, ssem, rsem, peer):
        return pltpu.make_async_remote_copy(src_ref=src, dst_ref=dst, send_sem=ssem, recv_sem=rsem,
                                            device_id=peer, device_id_type=MESH)

    sent = []

    def send(*what):
        copy = remote(*what)
        copy.start()
        sent.append(copy)
        return copy

    def received(copies):
        for copy in copies:
            copy.wait_recv()

    first, count = own_rows(counts_ref, n_mix)
    slot = lax.broadcasted_iota(jnp.int32, (8, capacity), 1)
    row = lax.broadcasted_iota(jnp.int32, (8, capacity), 0)
    sign = jnp.where(slot < count, 2 * bits_ref[...] - 1, 0)
    table = []
    for base in range(0, picks, 8):
        sample = jnp.zeros((8, capacity), jnp.int32)
        for i in range(8):
            sample = jnp.where(row == i, samples_ref[0, base + i], sample)
        odd = jnp.bitwise_and(sample, first + slot)
        for shift in (8, 4, 2, 1):
            odd = jnp.bitwise_xor(odd, jnp.right_shift(odd, shift))
        table.append(jnp.where(jnp.bitwise_and(odd, 1) == 1, -sign, sign))
    table = jnp.concatenate(table, axis=0).astype(jnp.float32).astype(jnp.bfloat16)
    scale = 1.0 / math.sqrt(n_mix * 128 * picks)
    for b in range(n_mix):
        rest_of = x_ref[:, 128 * b:128 * b + 128]
        total = None
        for _ in range(3):
            term = rest_of.astype(jnp.bfloat16)
            rest_of = rest_of - term.astype(jnp.float32)
            product = lax.dot_general(table, term, NN, preferred_element_type=jnp.float32)
            total = product if total is None else total + product
        part[b] = total * scale
    pl.semaphore_wait(barrier, n_mix - 1 + 2 * (n - 1))

    got = []
    for d in range(1, n_mix):
        p = (m + d) % n_mix
        got.append(send(part.at[p], r1.at[m], s1.at[d], v1.at[d], mix_peer(d)))
    r1[m] = part[m]
    a_ref[...] = jnp.zeros_like(a_ref)
    tp_ref[...] = jnp.zeros_like(tp_ref)
    z_ref[...] = jnp.zeros_like(z_ref)
    received(got)
    s_all[m] = functools.reduce(jnp.add, [r1[b] for b in range(n_mix)])
    received([send(s_all.at[m], s_all.at[m], s2.at[d], v2.at[d], mix_peer(d)) for d in range(1, n_mix)])

    def tiles(k):
        start, many = WAVES[k]
        for s in range(start, start + many):
            own = [TILES[min(n_mix * s + b, len(TILES) - 1)] for b in range(n_mix)]
            i = sum(own[b][0] * is_equal(m, b) for b in range(n_mix))
            j = sum(own[b][1] * is_equal(m, b) for b in range(n_mix))
            tile = lax.dot_general(s_all[i], s_all[j], TN, precision=HI, preferred_element_type=jnp.float32)
            for h in range(2):
                for p in range(n):
                    r = (h * n + p) * piece
                    w[k][h, p, s - start] = tile[r:r + piece]

    def reduce_first(k):
        got = []
        for d in range(1, n):
            got.append(send(w[k].at[0, (y + d) % n], r3[k].at[0, y], s3.at[k, 0, d], v3.at[k, 0, d], y_peer(d)))
            got.append(send(w[k].at[1, (z + d) % n], r3[k].at[1, z], s3.at[k, 1, d], v3.at[k, 1, d], z_peer(d)))
        r3[k][0, y] = w[k][0, y]
        r3[k][1, z] = w[k][1, z]
        return got

    def reduce_second(k, got):
        received(got)
        for h in range(2):
            q[k][h] = functools.reduce(jnp.add, [r3[k][h, p] for p in range(n)])
        got = []
        for d in range(1, n):
            got.append(send(q[k].at[0], r4[k].at[0, z], s4.at[k, 0, d], v4.at[k, 0, d], z_peer(d)))
            got.append(send(q[k].at[1], r4[k].at[1, y], s4.at[k, 1, d], v4.at[k, 1, d], y_peer(d)))
        r4[k][0, z] = q[k][0]
        r4[k][1, y] = q[k][1]
        return got

    def gather_mix(k, got):
        received(got)
        for h in range(2):
            f[k][h, m] = functools.reduce(jnp.add, [r4[k][h, p] for p in range(n)])
        got = []
        for d in range(nx):
            column = ((x + d) % nx) * 2
            if d:
                got.append(send(f[k].at[core, m], f[k].at[core, m], s5.at[k, 0, d], v5.at[k, 0, d], (dp, column + core)))
            got.append(send(f[k].at[1 - core, m], f[k].at[1 - core, m], s5.at[k, 1, d], v5.at[k, 1, d], (dp, column + 1 - core)))
        return got

    place = y + core * (z - y)
    sibling = (dp, m + 1 - 2 * core)

    def source(k):
        start, many = PASSES[k]
        return f0.at[core] if k == 0 else f1.at[core, :, pl.ds(start - 1, many)]

    def block(k, d):
        start, many = PASSES[k]
        return g_ref.at[core, (place + n - d) % n, :, pl.ds(start, many)]

    def place_copy(k, d):
        peer = (((y + d * (1 - core)) % n) * n + (z + d * core) % n, m)
        return remote(source(k), block(k, 0), s6.at[k, d], v6.at[k, d], peer)

    def own_copy(k):
        return pltpu.make_async_copy(source(k), block(k, 0), local.at[k])

    def core_copy(k, d):
        return remote(block(k, d) if d else source(k), block(k, d), s7.at[k, d], v7.at[k, d], sibling)

    def gather_places(k):
        for d in range(1, n):
            place_copy(k, d).start()
        core_copy(k, 0).start()
        own_copy(k).start()

    def pass_on(k):
        for d in range(1, n):
            place_copy(k, d).wait_recv()
            core_copy(k, d).start()

    def absorb(k):
        own_copy(k).wait()
        for d in range(n):
            core_copy(k, d).wait_recv()
        start, many = PASSES[k]
        for s in range(start, start + many):
            for b in range(n_mix):
                if n_mix * s + b < len(TILES):
                    i, j = TILES[n_mix * s + b]
                    for h in range(2):
                        for p in range(n):
                            r = i * 128 + (h * n + p) * piece
                            a_ref[r:r + piece, 128 * j:128 * j + 128] = a_ref[r:r + piece, 128 * j:128 * j + 128] + g_ref[h, p, b, s]

    tiles(0)
    early = reduce_first(0)
    tiles(1)
    late = reduce_first(1)
    early = reduce_second(0, early)
    late = reduce_second(1, late)
    early = gather_mix(0, early)
    received(early)
    gather_places(0)
    late = gather_mix(1, late)
    received(late)
    for k in range(1, len(PASSES)):
        gather_places(k)
    pass_on(0)
    absorb(0)
    d_ref[...] = a_ref[:128, :128]

    def step(kb, carry):
        past = pl.multiple_of((kb - 1) * 128, 128)
        here = pl.multiple_of(kb * 128, 128)
        col = a_ref[:, pl.ds(past, 128)]
        row_ids = lax.broadcasted_iota(jnp.int32, (size, 128), 0)
        mine = row_ids >= here
        v = jnp.where(mine, wide(left_terms(col), tr_ref[...]), 0.0)
        a_ref[:, pl.ds(past, 128)] = jnp.where(mine, v, col)
        vl_ref[...] = left_terms(v)
        vr_ref[...] = right_terms(v)
        for left in range(0, size, 256):
            update = wide(vl_ref[left:, :], vr_ref[left:left + 256, :])
            a_ref[left:, left:left + 256] = a_ref[left:, left:left + 256] - update
        return factor(kb, carry)

    def factor(kb, carry):
        factor_inverse(d_ref, t_ref, z_ref[...])
        tri = t_ref[...]
        half = pl.multiple_of((kb % 2) * 128, 128)
        tp_ref[kb // 2, pl.ds(half, 128), pl.ds(half, 128)] = tri
        tr_ref[...] = right_terms(tri)

        return carry

    def next_block(kb, carry):
        here = pl.multiple_of(kb * 128, 128)
        then = pl.multiple_of(jnp.minimum(kb + 1, nb - 1) * 128, 128)
        v = wide(left_terms(a_ref[pl.ds(then, 128), pl.ds(here, 128)]), tr_ref[...])
        d_ref[...] = a_ref[pl.ds(then, 128), pl.ds(then, 128)] - wide(left_terms(v), right_terms(v))
        return carry

    for kb in range(3):
        lax.fori_loop(kb, kb + 1, step if kb else factor, 0)
        pass_on(kb + 1)
        if kb == 0:
            absorb(1)
        if kb == 2:
            absorb(2)
        next_block(kb, 0)
    lax.fori_loop(3, 4, step, 0)
    absorb(3)
    next_block(3, 0)
    lax.fori_loop(4, nb, lambda kb, carry: next_block(kb, step(kb, carry)), 0)
    for p in range(nb // 2):
        s = 256 * p
        link = mm3(a_ref[s + 128:s + 256, s:s + 128], tp_ref[p, :128, :128], NN)
        tp_ref[p, 128:, :128] = -mm3(tp_ref[p, 128:, 128:], link, NN)
    acc_ref[...] = gt_ref[...]
    for p in range(nb // 2 - 1, -1, -1):
        s = slice(256 * p, 256 * p + 256)
        solved = mm3(acc_ref[:, s], tp_ref[p], NN)
        xt_ref[:, s] = solved
        if p:
            acc_ref[:, :256 * p] = acc_ref[:, :256 * p] - mm3(solved, a_ref[s, :256 * p], NN)
    proj = mm3(xt_ref[...], x_ref[...], NT)
    slot = lax.broadcasted_iota(jnp.int32, o_ref.shape, 1)
    o_ref[...] = jnp.where(slot < count, jnp.sum(proj * proj, axis=0, keepdims=True), 0.0)
    for copy in sent:
        copy.wait_send()
    for k in range(len(PASSES)):
        for d in range(n):
            if d:
                place_copy(k, d).wait_send()
            core_copy(k, d).wait_send()


def fused_call(n_mix, n, counts, samples, bits, x, gt):
    vm = pl.BlockSpec(memory_space=pltpu.VMEM)
    sm = pl.BlockSpec(memory_space=pltpu.SMEM)
    piece, k = 128 // (2 * n), samples.shape[1]
    f32, bf16 = jnp.float32, jnp.bfloat16
    dma = pltpu.SemaphoreType.DMA
    pair = lambda *s: [dma(s), dma(s)]
    waves = lambda *s: [pltpu.VMEM((*s, many, piece, 128), f32) for _, many in WAVES]
    return pl.pallas_call(
        functools.partial(fused_kernel, n_mix, n),
        out_shape=jax.ShapeDtypeStruct((1, x.shape[0]), f32),
        in_specs=[sm, sm, vm, vm, vm], out_specs=vm,
        scratch_shapes=[
            pltpu.VMEM((2, n, n_mix, SLOTS, piece, 128), f32),
            pltpu.VMEM((n_mix, k, 128), f32), pltpu.VMEM((n_mix, k, 128), f32), pltpu.VMEM((n_mix, k, 128), f32),
            *waves(2, n), *waves(2, n), *waves(2), *waves(2, n), *waves(2, n_mix),
            *pair(n_mix), *pair(n_mix), *pair(2, 2, n), *pair(2, 2, n), *pair(2, 2, n_mix // 2),
            *pair(len(PASSES), n), *pair(len(PASSES), n), dma((len(PASSES),)),
            pltpu.VMEM((1024, 1024), f32), pltpu.VMEM((4, 256, 256), f32), pltpu.VMEM((128, 128), f32),
            pltpu.VMEM((128, 128), f32), pltpu.VMEM((64, 1024), f32), pltpu.VMEM((64, 1024), f32),
            pltpu.VMEM((128, 768), bf16), pltpu.VMEM((1024, 768), bf16), pltpu.VMEM((1024, 768), bf16),
            pltpu.VMEM((8, 128), f32)],
        compiler_params=pltpu.CompilerParams(collective_id=0, has_side_effects=True, vmem_limit_bytes=48 * 1024 * 1024),
    )(counts, samples, bits, x, gt)


def shards(matrix, counts, sign_bits, samples, gaussian):
    n_mix, n_dp = lax.axis_size("mix"), lax.axis_size("dp")
    return fused_call(n_mix, math.isqrt(n_dp), counts, samples, sign_bits[None, :], matrix, gaussian.T)[0]


def solution(mesh):
    in_specs = (P(("dp", "mix"), None), P("dp", None), P(("dp", "mix")), P("dp", None), P())
    out_specs = P(("dp", "mix"))
    return jax.shard_map(shards, mesh=mesh, in_specs=in_specs, out_specs=out_specs, check_vma=False)
```
